32 devices in a mesh: fibre: 2 (over y), chan: 4 (over z), win: 2 (over x), freq: 2 (over core).
Axes of the slice: x: 2, y: 2, z: 4, core: 2. Of those that a mesh axis runs over, the one named last changes fastest.
Arguments:
- spectra: bfloat16 [16, 2, 64, 2048], P('win', None, ('fibre', 'chan'), 'freq'), parts along dimension 2, may hold values from -50 to 50
- keep: int32 [32], P(('fibre', 'win')), parts along dimension 0, may hold values 0 or 1
- pair_mask: int32 [64, 4], P(('fibre', 'chan')), parts along dimension 0, may hold values 0 or 1
Outputs:
- correlations: float32 [64, 4, 8, 1024], P(('fibre', 'chan'), None, None, ('win', 'freq')), parts along dimension 0
The draws below stay inside these ranges and needn't reach their ends.
There are 2 independent parts, one for each index of `fibre`. The reference program is written for one: setup_inputs(seed, part) draws one part's arguments, and reference() takes and returns one part's arrays. A program takes and returns all parts, laid end to end along the dimension named above; each array names one. Nothing has to cross between parts.
All inputs are finite; a program needn't handle non-finite values. No bound on the sum of `keep` or of `pair_mask` on one device may be relied on, other than what follows from the above.
Results may differ from the reference program's by a relative error of at most 0.0014.
Values may be sent and summed in bfloat16 or wider, within the bound.
A program may use at most 128 MiB of HBM per device.

```python
import math
import jax
import jax.numpy as jnp
from jax import lax

F = 2048
LAGS = 1024
F_LO = 60
NSAMP = 15000
CH_DEV = 8
CH = 32
W = 16
CYCLE = 3


def draw_spectra(key, part):
    base_key, scale_key = jax.random.split(jax.random.fold_in(key, 17))
    quarter = jnp.arange(F) * 4 // F
    base = jnp.clip(jax.random.normal(base_key, (W, 2, CH, F), jnp.float32), -5.0, 5.0)
    levels = jnp.exp(jax.random.uniform(scale_key, (W, 1, CH, 4), jnp.float32) * math.log(10.0))
    scales = levels[:, :, :, quarter]
    return (base * scales).astype(jnp.bfloat16)


def set_ends(array, rng, least, high):
    place = [jax.random.randint(jax.random.fold_in(rng, axis), (), 0, length) for axis, length in enumerate(array.shape)]
    longest = array.shape.index(max(array.shape))
    next_to = place[:longest] + [(place[longest] + 1) % array.shape[longest]] + place[longest + 1:]
    return array.at[tuple(place)].set(least).at[tuple(next_to)].set(high)


def setup_inputs(seed: int = 0, part: int = 0) -> dict:
    keys = jax.random.split(jax.random.key(seed), 4)
    part_splits = jax.random.split(jax.random.fold_in(keys[3], part), 4)
    return {
        "spectra": draw_spectra(jax.random.fold_in(jax.random.fold_in(keys[3], part), 71), part),
        "keep": set_ends((jax.random.randint(part_splits[1], (W,), 0, 4) < 3).astype(jnp.int32), jax.random.fold_in(part_splits[1], 1), 0, 1),
        "pair_mask": set_ends((jax.random.randint(part_splits[2], (CH, CYCLE + 1), 0, 5) < 4).astype(jnp.int32), jax.random.fold_in(part_splits[2], 1), 0, 1),
    }


EPS = 1e-06

def lag_table(start, count):
    bins = F_LO + start + jnp.arange(count, dtype=jnp.int32)
    offsets = jnp.arange(LAGS, dtype=jnp.int32) - LAGS // 2
    turns = jnp.remainder(bins[:, None] * offsets[None, :], NSAMP).astype(jnp.float32)
    angle = turns * (2.0 * math.pi / NSAMP)
    return jnp.concatenate([jnp.cos(angle), -jnp.sin(angle)], axis=0)

def reference(spectra, keep, pair_mask):
    spec = spectra.astype(jnp.float32)
    power = lax.optimization_barrier(jnp.sum(spec * spec, axis=(1, 3))) / F
    white = lax.optimization_barrier((spec * lax.rsqrt(power + EPS)[:, None, :, None]).astype(jnp.bfloat16))
    white = white.astype(jnp.float32)
    own = white * keep.astype(jnp.float32)[:, None, None, None]
    swapped = jnp.concatenate([own[:, 1:2], -own[:, 0:1]], axis=1)
    blocks = CH // CH_DEV
    padded = jnp.concatenate([white, jnp.zeros((W, 2, CYCLE * CH_DEV, F), jnp.float32)], axis=2)
    table = lag_table(0, F)
    own_blocks = own.reshape(W, 2, blocks, CH_DEV, F)
    swap_blocks = swapped.reshape(W, 2, blocks, CH_DEV, F)

    def one_offset(step):
        partner = lax.dynamic_slice_in_dim(padded, (step * CH_DEV).astype(jnp.int32), CH, 2)
        partner = partner.reshape(W, 2, blocks, CH_DEV, F)
        real_part = jnp.einsum('wcbif,wcbjf->bijf', own_blocks, partner)
        imag_part = jnp.einsum('wcbif,wcbjf->bijf', swap_blocks, partner)
        cross = jnp.concatenate([real_part, imag_part], axis=-1).reshape(CH * CH_DEV, 2 * F)
        lagsum = jnp.dot(cross, table, precision=lax.Precision.HIGHEST)
        return lagsum.reshape(CH, CH_DEV, LAGS)
    stacked = lax.map(one_offset, jnp.arange(CYCLE + 1, dtype=jnp.int32))
    lagsum = jnp.transpose(stacked, (1, 0, 2, 3))
    scale = 1.0 / math.sqrt(W * F)
    return lagsum * scale * pair_mask.astype(jnp.float32)[:, :, None, None]
```

```python
import functools
import math

import jax
import jax.numpy as jnp
import numpy as np
from jax import lax
from jax.experimental import pallas as pl
from jax.experimental.pallas import tpu as pltpu
from jax.sharding import PartitionSpec as P

LAGS = 1024
F_LO = 60
NSAMP = 15000
EPS = 1e-06
LANES = 128
FINE = 16
MESH = pl.DeviceIdType.MESH


def turn_table(bins):
    offsets = np.arange(LAGS, dtype=np.int64) - LAGS // 2
    turns = np.remainder(np.asarray(bins, np.int64)[:, None] * offsets[None, :], NSAMP)
    angle = turns.astype(np.float64) * (2.0 * math.pi / NSAMP)
    return np.stack([np.cos(angle), np.sin(angle)]).astype(np.float32)


def split(x):
    high = x.astype(jnp.bfloat16)
    low = (x - high.astype(jnp.float32)).astype(jnp.bfloat16)
    return high, low


def kernel(reach, sizes, keep_ref, spec_ref, coarse_ref, fine_ref, out_ref,
           comm, own, power, power_in, coarse, table, lhs, partial, arrived,
           load_sem, power_send, power_recv, block_send, block_recv, sum_send, sum_recv):
    n_chan, n_win, n_freq = sizes
    w_dev, _, ch_dev, f_dev = spec_ref.shape
    chan, win, freq = (lax.axis_index(name) for name in ("chan", "win", "freq"))
    n_group = n_win * n_freq
    me = win * n_freq + freq
    lag_dev = LAGS // n_group
    rows = ch_dev * ch_dev

    def peer(step):
        g = lax.rem(me + step, n_group)
        return g, {"win": g // n_freq, "freq": lax.rem(g, n_freq)}

    barrier = pltpu.get_barrier_semaphore()
    for step in range(1, n_group):
        pl.semaphore_signal(barrier, inc=1, device_id=peer(step)[1], device_id_type=MESH)

    @pl.when(chan > 0)
    def _():
        pl.semaphore_signal(barrier, inc=1, device_id={"chan": chan - 1}, device_id_type=MESH)

    @pl.when(chan < n_chan - 1)
    def _():
        pl.semaphore_signal(barrier, inc=1, device_id={"chan": chan + 1}, device_id_type=MESH)

    groups = f_dev // FINE
    load = pltpu.make_async_copy(
        coarse_ref.at[:, pl.ds(pl.multiple_of(freq * groups, groups), groups)], coarse, load_sem)
    load.start()

    for w in range(w_dev):
        x = spec_ref[w].astype(jnp.float32)
        s = x[0] * x[0] + x[1] * x[1]
        total = s[:, :LANES]
        for q in range(1, f_dev // LANES):
            total = total + s[:, q * LANES:(q + 1) * LANES]
        power[w] = total

    inside = jnp.where(chan > 0, 1, 0) + jnp.where(chan < n_chan - 1, 1, 0)
    pl.semaphore_wait(barrier, n_group - 1 + inside)

    power_copies = []
    for step in range(1, n_freq):
        copy = pltpu.make_async_remote_copy(
            src_ref=power, dst_ref=power_in.at[step - 1],
            send_sem=power_send.at[step - 1], recv_sem=power_recv.at[step - 1],
            device_id={"freq": lax.rem(freq + step, n_freq)}, device_id_type=MESH)
        copy.start()
        power_copies.append(copy)
    for copy in power_copies:
        copy.wait()

    for w in range(w_dev):
        total = power[w]
        for step in range(1, n_freq):
            total = total + power_in[step - 1, w]
        mean = jnp.sum(total, axis=-1, keepdims=True) / (f_dev * n_freq)
        white = (spec_ref[w].astype(jnp.float32) * lax.rsqrt(mean + EPS)[None]).astype(jnp.bfloat16)
        comm[0, w] = white
        own[w] = white.astype(jnp.float32) * keep_ref[w].astype(jnp.float32)

    def block_copy(k):
        return pltpu.make_async_remote_copy(
            src_ref=comm.at[k], dst_ref=comm.at[k + 1],
            send_sem=block_send.at[k], recv_sem=block_recv.at[k],
            device_id={"chan": chan - 1}, device_id_type=MESH)

    @pl.when(chan > 0)
    def _():
        block_copy(0).start()

    load.wait()

    def make_table(a, carry):
        fine_cos, fine_sin = fine_ref[0], fine_ref[1]
        coarse_cos, coarse_sin = coarse[0, pl.ds(a, 1)], coarse[1, pl.ds(a, 1)]
        cos = coarse_cos * fine_cos - coarse_sin * fine_sin
        minus_sin = -(coarse_sin * fine_cos) - coarse_cos * fine_sin
        per = LANES // FINE
        row = pl.multiple_of((a // per) * (2 * LANES) + lax.rem(a, per) * FINE, FINE)
        for value, at in ((cos, row), (minus_sin, row + LANES)):
            high, low = split(value)
            at = pl.ds(pl.multiple_of(at, FINE), FINE)
            table[0, at] = high
            table[1, at] = low
        return carry

    lax.fori_loop(0, groups, make_table, 0)

    def sum_copy(k, step):
        g, where = peer(step)
        return pltpu.make_async_remote_copy(
            src_ref=partial.at[k, g], dst_ref=arrived.at[k, step - 1],
            send_sem=sum_send.at[k, step - 1], recv_sem=sum_recv.at[k, step - 1],
            device_id=where, device_id_type=MESH)

    def one_offset(k, carry):
        @pl.when(jnp.logical_and(k > 0, chan + k < n_chan))
        def _():
            block_copy(k - 1).wait_recv()

        @pl.when(jnp.logical_and(jnp.logical_and(k > 0, k < reach), jnp.logical_and(chan > 0, chan + k < n_chan)))
        def _():
            block_copy(k).start()

        @pl.when(chan + k < n_chan)
        def _():
            def cross(q, c):
                lanes = pl.ds(pl.multiple_of(q * LANES, LANES), LANES)
                partner = comm[k, :, :, :, lanes].astype(jnp.float32)
                for i in range(0, ch_dev, 2):
                    real, imag = [], []
                    for ii in (i, i + 1):
                        re = im = None
                        for w in range(w_dev):
                            a = jnp.broadcast_to(own[w, 0, pl.ds(ii, 1), lanes], (ch_dev, LANES))
                            b = jnp.broadcast_to(own[w, 1, pl.ds(ii, 1), lanes], (ch_dev, LANES))
                            p, r = partner[w, 0], partner[w, 1]
                            one, two = a * p + b * r, b * p - a * r
                            re = one if re is None else re + one
                            im = two if im is None else im + two
                        real.append(re)
                        imag.append(im)
                    for part, value in enumerate((real, imag)):
                        high, low = split(jnp.concatenate(value, axis=0))
                        at = pl.ds(pl.multiple_of(q * 2 * LANES + part * LANES, LANES), LANES)
                        lhs[pl.ds(i * ch_dev, 2 * ch_dev), at] = high
                        lhs[pl.ds(rows + i * ch_dev, 2 * ch_dev), at] = low
                return c

            lax.fori_loop(0, f_dev // LANES, cross, 0)
            for step in list(range(1, n_group)) + [0]:
                g, _ = peer(step)
                lags = pl.ds(pl.multiple_of(g * lag_dev, lag_dev), lag_dev)
                both = jnp.dot(lhs[...], table[0, :, lags], preferred_element_type=jnp.float32)
                rest = jnp.dot(lhs[pl.ds(0, rows)], table[1, :, lags], preferred_element_type=jnp.float32)
                partial[k, g] = both[:rows] + (both[rows:] + rest)
                if step:
                    sum_copy(k, step).start()

        return carry

    lax.fori_loop(0, reach + 1, one_offset, 0)

    for k in range(reach + 1):
        @pl.when(chan + k < n_chan)
        def _():
            total = partial[k, me]
            for step in range(1, n_group):
                sum_copy(k, step).wait_recv()
                total = total + arrived[k, step - 1]
            out_ref[:, k] = total.reshape(ch_dev, ch_dev, lag_dev)

        @pl.when(chan + k >= n_chan)
        def _():
            out_ref[:, k] = jnp.zeros((ch_dev, ch_dev, lag_dev), jnp.float32)

    for k in range(reach + 1):
        @pl.when(chan + k < n_chan)
        def _():
            for step in range(1, n_group):
                sum_copy(k, step).wait_send()

        if k < reach:
            @pl.when(jnp.logical_and(chan > 0, chan + k < n_chan))
            def _():
                block_copy(k).wait_send()


def local(spectra, keep, pair_mask):
    w_dev, _, ch_dev, f_dev = spectra.shape
    reach = pair_mask.shape[1] - 1
    n_chan, n_freq, n_win = (lax.axis_size(name) for name in ("chan", "freq", "win"))
    n_group = n_freq * n_win
    lag_dev = LAGS // n_group
    rows = ch_dev * ch_dev
    coarse = jnp.asarray(turn_table(F_LO + np.arange(0, f_dev * n_freq, FINE)))
    fine = jnp.asarray(turn_table(np.arange(FINE)))
    groups = f_dev // FINE
    vmem = pl.BlockSpec(memory_space=pltpu.VMEM)
    dma = pltpu.SemaphoreType.DMA
    lagsum = pl.pallas_call(
        functools.partial(kernel, reach, (n_chan, n_win, n_freq)),
        out_shape=jax.ShapeDtypeStruct((ch_dev, reach + 1, ch_dev, lag_dev), jnp.float32),
        in_specs=[pl.BlockSpec(memory_space=pltpu.SMEM), vmem, pl.BlockSpec(memory_space=pl.ANY), vmem],
        out_specs=vmem,
        scratch_shapes=[
            pltpu.VMEM((reach + 1,) + spectra.shape, jnp.bfloat16),
            pltpu.VMEM(spectra.shape, jnp.float32),
            pltpu.VMEM((w_dev, ch_dev, LANES), jnp.float32),
            pltpu.VMEM((n_freq - 1, w_dev, ch_dev, LANES), jnp.float32),
            pltpu.VMEM((2, groups, LAGS), jnp.float32),
            pltpu.VMEM((2, 2 * f_dev, LAGS), jnp.bfloat16),
            pltpu.VMEM((2 * rows, 2 * f_dev), jnp.bfloat16),
            pltpu.VMEM((reach + 1, n_group, rows, lag_dev), jnp.float32),
            pltpu.VMEM((reach + 1, n_group - 1, rows, lag_dev), jnp.float32),
            dma,
            dma((n_freq - 1,)),
            dma((n_freq - 1,)),
            dma((reach,)),
            dma((reach,)),
            dma((reach + 1, n_group - 1)),
            dma((reach + 1, n_group - 1)),
        ],
        compiler_params=pltpu.CompilerParams(
            collective_id=0, has_side_effects=True, vmem_limit_bytes=60 * 1024 * 1024),
    )(keep, spectra, coarse, fine)
    scale = 1.0 / math.sqrt(w_dev * n_win * f_dev * n_freq)
    return lagsum * scale * pair_mask.astype(jnp.float32)[:, :, None, None]


def solution(mesh):
    in_specs = (
        P("win", None, ("fibre", "chan"), "freq"),
        P(("fibre", "win")),
        P(("fibre", "chan"), None),
    )
    out_specs = P(("fibre", "chan"), None, None, ("win", "freq"))
    return jax.shard_map(local, mesh=mesh, in_specs=in_specs, out_specs=out_specs, check_vma=False)
```

```python
import functools
import math

import jax
import jax.numpy as jnp
import numpy as np
from jax import lax
from jax.experimental import pallas as pl
from jax.experimental.pallas import tpu as pltpu
from jax.sharding import PartitionSpec as P

LAGS = 1024
F_LO = 60
NSAMP = 15000
EPS = 1e-06
LANES = 128
FINE = 16
PIECES = 4
EARLY = 2
MESH = pl.DeviceIdType.MESH


def turn_table(bins):
    offsets = np.arange(LAGS, dtype=np.int64) - LAGS // 2
    turns = np.remainder(np.asarray(bins, np.int64)[:, None] * offsets[None, :], NSAMP)
    angle = turns.astype(np.float64) * (2.0 * math.pi / NSAMP)
    return np.stack([np.cos(angle), np.sin(angle)]).astype(np.float32)


def split(x):
    high = x.astype(jnp.bfloat16)
    low = (x - high.astype(jnp.float32)).astype(jnp.bfloat16)
    return high, low


def kernel(reach, sizes, keep_ref, mask_ref, spec_ref, coarse_ref, fine_ref, out_ref,
           comm, scales, gains, own, power, power_in, coarse, fine, table, lhs, partial, arrived, result,
           spec_sem, load_sem, out_sem, power_send, power_recv, scale_send, scale_recv, block_send, block_recv, sum_send, sum_recv):
    n_chan, n_win, n_freq = sizes
    w_dev, _, ch_dev, f_dev = spec_ref.shape
    chan, win, freq = (lax.axis_index(name) for name in ("chan", "win", "freq"))
    n_group = n_win * n_freq
    me = win * n_freq + freq
    lag_dev = LAGS // n_group
    rows = ch_dev * ch_dev
    f_piece = f_dev // PIECES
    scale = 1.0 / math.sqrt(w_dev * n_win * f_dev * n_freq)

    def peer(step):
        g = lax.rem(me + step, n_group)
        return g, {"win": g // n_freq, "freq": lax.rem(g, n_freq)}

    barrier = pltpu.get_barrier_semaphore()

    @pl.when(chan > 0)
    def _():
        pl.semaphore_signal(barrier, inc=1, device_id={"chan": chan - 1}, device_id_type=MESH)

    @pl.when(chan < n_chan - 1)
    def _():
        pl.semaphore_signal(barrier, inc=1, device_id={"chan": chan + 1}, device_id_type=MESH)

    for step in range(1, n_group):
        pl.semaphore_signal(barrier, inc=1, device_id=peer(step)[1], device_id_type=MESH)

    groups = f_dev // FINE
    loads = [pltpu.make_async_copy(
        spec_ref.at[:, :, :, pl.ds(c * f_piece, f_piece)], comm.at[0, c], spec_sem.at[c]) for c in range(PIECES)]
    tables = [
        pltpu.make_async_copy(
            coarse_ref.at[:, pl.ds(pl.multiple_of(freq * groups, groups), groups)], coarse, load_sem.at[0]),
        pltpu.make_async_copy(fine_ref, fine, load_sem.at[1])]
    for load in loads + tables:
        load.start()

    inside = jnp.where(chan > 0, 1, 0) + jnp.where(chan < n_chan - 1, 1, 0)
    pl.semaphore_wait(barrier, n_group - 1 + inside)

    def piece_copy(k, c, source=None):
        return pltpu.make_async_remote_copy(
            src_ref=comm.at[k, c] if source is None else source.at[:, :, :, pl.ds(c * f_piece, f_piece)],
            dst_ref=comm.at[k + 1, c],
            send_sem=block_send.at[k, c], recv_sem=block_recv.at[k, c],
            device_id={"chan": chan - 1}, device_id_type=MESH)

    def scale_copy(k):
        return pltpu.make_async_remote_copy(
            src_ref=scales.at[k], dst_ref=scales.at[k + 1],
            send_sem=scale_send.at[k], recv_sem=scale_recv.at[k],
            device_id={"chan": chan - 1}, device_id_type=MESH)

    @pl.when(chan > 0)
    def _():
        for c in range(EARLY):
            piece_copy(0, c, spec_ref).start()

    for load in loads:
        load.wait()

    for w in range(w_dev):
        total = None
        for c in range(PIECES):
            x = comm[0, c, w].astype(jnp.float32)
            s = x[0] * x[0] + x[1] * x[1]
            for q in range(f_piece // LANES):
                term = s[:, q * LANES:(q + 1) * LANES]
                total = term if total is None else total + term
        power[w] = total

    power_copies = []
    for step in range(1, n_freq):
        copy = pltpu.make_async_remote_copy(
            src_ref=power, dst_ref=power_in.at[step - 1],
            send_sem=power_send.at[step - 1], recv_sem=power_recv.at[step - 1],
            device_id={"freq": lax.rem(freq + step, n_freq)}, device_id_type=MESH)
        copy.start()
        power_copies.append(copy)

    for copy in power_copies:
        copy.wait()

    lane = lax.broadcasted_iota(jnp.int32, (ch_dev, LANES), 1)
    tile = jnp.zeros((ch_dev, LANES), jnp.float32)
    for w in range(w_dev):
        total = power[w]
        for step in range(1, n_freq):
            total = total + power_in[step - 1, w]
        mean = jnp.sum(total, axis=-1, keepdims=True) / (f_dev * n_freq)
        tile = jnp.where(lane == w, lax.rsqrt(mean + EPS), tile)
    scales[0] = tile

    @pl.when(chan > 0)
    def _():
        scale_copy(0).start()
        for c in range(EARLY, PIECES):
            piece_copy(0, c, spec_ref).start()

    def spread(k):
        tile = scales[k]
        for w in range(w_dev):
            gains[w] = jnp.broadcast_to(tile[:, w:w + 1], (ch_dev, LANES))

    spread(0)
    for w in range(w_dev):
        gain = jnp.concatenate([gains[w]] * (f_piece // LANES), axis=1)
        kept = keep_ref[w].astype(jnp.float32)
        for c in range(PIECES):
            white = (comm[0, c, w].astype(jnp.float32) * gain[None]).astype(jnp.bfloat16)
            own[w, :, :, pl.ds(c * f_piece, f_piece)] = white.astype(jnp.float32) * kept

    for load in tables:
        load.wait()

    def make_table(a, carry):
        fine_cos, fine_sin = fine[0], fine[1]
        coarse_cos, coarse_sin = coarse[0, pl.ds(a, 1)], coarse[1, pl.ds(a, 1)]
        cos = coarse_cos * fine_cos - coarse_sin * fine_sin
        minus_sin = -(coarse_sin * fine_cos) - coarse_cos * fine_sin
        per = LANES // FINE
        row = pl.multiple_of((a // per) * (2 * LANES) + lax.rem(a, per) * FINE, FINE)
        for value, at in ((cos, row), (minus_sin, row + LANES)):
            high, low = split(value)
            at = pl.ds(pl.multiple_of(at, FINE), FINE)
            table[0, at] = high
            table[1, at] = low
        return carry

    lax.fori_loop(0, groups, make_table, 0)

    def sum_copy(k, step):
        g, where = peer(step)
        return pltpu.make_async_remote_copy(
            src_ref=partial.at[k, g], dst_ref=arrived.at[k, step - 1],
            send_sem=sum_send.at[k, step - 1], recv_sem=sum_recv.at[k, step - 1],
            device_id=where, device_id_type=MESH)

    def receive(k, pieces, with_scale):
        @pl.when(chan + k < n_chan)
        def _():
            onward = jnp.logical_and(k < reach, chan > 0)
            for c in pieces:
                piece_copy(k - 1, c).wait_recv()

                @pl.when(onward)
                def _():
                    piece_copy(k, c).start()

            if with_scale:
                scale_copy(k - 1).wait_recv()

                @pl.when(onward)
                def _():
                    scale_copy(k).start()

    def compute(k, first, last):
        start = first * f_piece
        depth = (last - first) * f_piece

        def cross(q, c):
            lanes = pl.ds(pl.multiple_of(start + q * LANES, LANES), LANES)
            per = f_piece // LANES
            piece = first + q // per
            within = pl.ds(pl.multiple_of(lax.rem(q, per) * LANES, LANES), LANES)
            partner = []
            for w in range(w_dev):
                white = comm[k, piece, w, :, :, within].astype(jnp.float32) * gains[w][None]
                partner.append(white.astype(jnp.bfloat16).astype(jnp.float32))
            for i in range(0, ch_dev, 2):
                real, imag = [], []
                for ii in (i, i + 1):
                    re = im = None
                    for w in range(w_dev):
                        a = jnp.broadcast_to(own[w, 0, pl.ds(ii, 1), lanes], (ch_dev, LANES))
                        b = jnp.broadcast_to(own[w, 1, pl.ds(ii, 1), lanes], (ch_dev, LANES))
                        p, r = partner[w][0], partner[w][1]
                        one, two = a * p + b * r, b * p - a * r
                        re = one if re is None else re + one
                        im = two if im is None else im + two
                    real.append(re)
                    imag.append(im)
                for part, value in enumerate((real, imag)):
                    high, low = split(jnp.concatenate(value, axis=0))
                    at = pl.ds(pl.multiple_of(2 * start + q * 2 * LANES + part * LANES, LANES), LANES)
                    lhs[pl.ds(i * ch_dev, 2 * ch_dev), at] = high
                    lhs[pl.ds(rows + i * ch_dev, 2 * ch_dev), at] = low
            return c

        lax.fori_loop(0, depth // LANES, cross, 0)
        deep = pl.ds(2 * start, 2 * depth)
        for step in list(range(1, n_group)) + [0]:
            g, _ = peer(step)
            lags = pl.ds(pl.multiple_of(g * lag_dev, lag_dev), lag_dev)
            both = jnp.dot(lhs[:, deep], table[0, deep, lags], preferred_element_type=jnp.float32)
            rest = jnp.dot(lhs[pl.ds(0, rows), deep], table[1, deep, lags], preferred_element_type=jnp.float32)
            value = both[:rows] + (both[rows:] + rest)
            partial[k, g] = value if first == 0 else partial[k, g] + value
            if step and last == PIECES:
                sum_copy(k, step).start()

    def out_copy(k):
        return pltpu.make_async_copy(result.at[k], out_ref.at[:, k], out_sem.at[k])

    def finish(k):
        @pl.when(chan + k < n_chan)
        def _():
            total = partial[k, me]
            for step in range(1, n_group):
                sum_copy(k, step).wait_recv()
                total = total + arrived[k, step - 1]
            for c in range(ch_dev):
                result[k, c] = total[c * ch_dev:(c + 1) * ch_dev] * (mask_ref[k, c].astype(jnp.float32) * scale)

        @pl.when(chan + k >= n_chan)
        def _():
            result[k] = jnp.zeros((ch_dev, ch_dev, lag_dev), jnp.float32)

        out_copy(k).start()

    receive(1, range(EARLY), True)

    def one_offset(k, carry):
        @pl.when(chan + k < n_chan)
        def _():
            spread(k)
            compute(k, 0, EARLY)

        for c in range(EARLY, PIECES):
            @pl.when(k > 0)
            def _():
                receive(k, (c,), False)

            @pl.when(chan + k < n_chan)
            def _():
                compute(k, c, c + 1)

        @pl.when(k > 0)
        def _():
            @pl.when(k < reach)
            def _():
                receive(k + 1, range(EARLY), True)

            finish(k - 1)

        return carry

    lax.fori_loop(0, reach + 1, one_offset, 0)
    finish(reach)

    for k in range(reach + 1):
        out_copy(k).wait()

        @pl.when(chan + k < n_chan)
        def _():
            for step in range(1, n_group):
                sum_copy(k, step).wait_send()

        if k < reach:
            @pl.when(jnp.logical_and(chan > 0, chan + k < n_chan))
            def _():
                scale_copy(k).wait_send()
                for c in range(PIECES):
                    piece_copy(k, c, spec_ref if k == 0 else None).wait_send()


def local(spectra, keep, pair_mask):
    w_dev, _, ch_dev, f_dev = spectra.shape
    reach = pair_mask.shape[1] - 1
    n_chan, n_freq, n_win = (lax.axis_size(name) for name in ("chan", "freq", "win"))
    n_group = n_freq * n_win
    lag_dev = LAGS // n_group
    rows = ch_dev * ch_dev
    coarse = jnp.asarray(turn_table(F_LO + np.arange(0, f_dev * n_freq, FINE)))
    fine = jnp.asarray(turn_table(np.arange(FINE)))
    groups = f_dev // FINE
    smem = pl.BlockSpec(memory_space=pltpu.SMEM)
    hbm = pl.BlockSpec(memory_space=pl.ANY)
    dma = pltpu.SemaphoreType.DMA
    return pl.pallas_call(
        functools.partial(kernel, reach, (n_chan, n_win, n_freq)),
        out_shape=jax.ShapeDtypeStruct((ch_dev, reach + 1, ch_dev, lag_dev), jnp.float32),
        in_specs=[smem, smem, hbm, hbm, hbm],
        out_specs=hbm,
        scratch_shapes=[
            pltpu.VMEM((reach + 1, PIECES, w_dev, 2, ch_dev, f_dev // PIECES), jnp.bfloat16),
            pltpu.VMEM((reach + 1, ch_dev, LANES), jnp.float32),
            pltpu.VMEM((w_dev, ch_dev, LANES), jnp.float32),
            pltpu.VMEM(spectra.shape, jnp.float32),
            pltpu.VMEM((w_dev, ch_dev, LANES), jnp.float32),
            pltpu.VMEM((n_freq - 1, w_dev, ch_dev, LANES), jnp.float32),
            pltpu.VMEM((2, groups, LAGS), jnp.float32),
            pltpu.VMEM((2, FINE, LAGS), jnp.float32),
            pltpu.VMEM((2, 2 * f_dev, LAGS), jnp.bfloat16),
            pltpu.VMEM((2 * rows, 2 * f_dev), jnp.bfloat16),
            pltpu.VMEM((reach + 1, n_group, rows, lag_dev), jnp.float32),
            pltpu.VMEM((reach + 1, n_group - 1, rows, lag_dev), jnp.float32),
            pltpu.VMEM((reach + 1, ch_dev, ch_dev, lag_dev), jnp.float32),
            dma((PIECES,)),
            dma((2,)),
            dma((reach + 1,)),
            dma((n_freq - 1,)),
            dma((n_freq - 1,)),
            dma((reach,)),
            dma((reach,)),
            dma((reach, PIECES)),
            dma((reach, PIECES)),
            dma((reach + 1, n_group - 1)),
            dma((reach + 1, n_group - 1)),
        ],
        compiler_params=pltpu.CompilerParams(
            collective_id=0, has_side_effects=True, vmem_limit_bytes=60 * 1024 * 1024),
    )(keep, pair_mask.T, spectra, coarse, fine)


def solution(mesh):
    in_specs = (
        P("win", None, ("fibre", "chan"), "freq"),
        P(("fibre", "win")),
        P(("fibre", "chan"), None),
    )
    out_specs = P(("fibre", "chan"), None, None, ("win", "freq"))
    return jax.shard_map(local, mesh=mesh, in_specs=in_specs, out_specs=out_specs, check_vma=False)
```

```python
import functools
import math

import jax
import jax.numpy as jnp
import numpy as np
from jax import lax
from jax.experimental import pallas as pl
from jax.experimental.pallas import tpu as pltpu
from jax.sharding import PartitionSpec as P

LAGS = 1024
F_LO = 60
NSAMP = 15000
EPS = 1e-06
LANES = 128
FINE = 16
PIECES = 4
EARLY = 2
MESH = pl.DeviceIdType.MESH


def turn_table(bins):
    offsets = np.arange(LAGS, dtype=np.int64) - LAGS // 2
    turns = np.remainder(np.asarray(bins, np.int64)[:, None] * offsets[None, :], NSAMP)
    angle = turns.astype(np.float64) * (2.0 * math.pi / NSAMP)
    return np.stack([np.cos(angle), np.sin(angle)]).astype(np.float32)


def split(x):
    high = x.astype(jnp.bfloat16)
    low = (x - high.astype(jnp.float32)).astype(jnp.bfloat16)
    return high, low


def kernel(reach, sizes, keep_ref, mask_ref, spec_ref, coarse_ref, fine_ref, out_ref,
           comm, scales, gains, own, power, power_in, coarse, fine, table, lhs, partial, arrived,
           spec_sem, load_sem, power_send, power_recv, scale_send, scale_recv, block_send, block_recv, sum_send, sum_recv):
    n_chan, n_win, n_freq = sizes
    w_dev, _, ch_dev, f_dev = spec_ref.shape
    chan, win, freq = (lax.axis_index(name) for name in ("chan", "win", "freq"))
    n_group = n_win * n_freq
    me = win * n_freq + freq
    lag_dev = LAGS // n_group
    rows = ch_dev * ch_dev
    f_piece = f_dev // PIECES
    scale = 1.0 / math.sqrt(w_dev * n_win * f_dev * n_freq)

    def peer(step):
        g = lax.rem(me + step, n_group)
        return g, {"win": g // n_freq, "freq": lax.rem(g, n_freq)}

    barrier = pltpu.get_barrier_semaphore()

    @pl.when(chan > 0)
    def _():
        pl.semaphore_signal(barrier, inc=1, device_id={"chan": chan - 1}, device_id_type=MESH)

    @pl.when(chan < n_chan - 1)
    def _():
        pl.semaphore_signal(barrier, inc=1, device_id={"chan": chan + 1}, device_id_type=MESH)

    for step in range(1, n_group):
        pl.semaphore_signal(barrier, inc=1, device_id=peer(step)[1], device_id_type=MESH)

    groups = f_dev // FINE
    loads = [pltpu.make_async_copy(
        spec_ref.at[:, :, :, pl.ds(c * f_piece, f_piece)], comm.at[0, c], spec_sem.at[c]) for c in range(PIECES)]
    tables = [
        pltpu.make_async_copy(
            coarse_ref.at[:, pl.ds(pl.multiple_of(freq * groups, groups), groups)], coarse, load_sem.at[0]),
        pltpu.make_async_copy(fine_ref, fine, load_sem.at[1])]
    for load in loads + tables:
        load.start()

    inside = jnp.where(chan > 0, 1, 0) + jnp.where(chan < n_chan - 1, 1, 0)
    pl.semaphore_wait(barrier, n_group - 1 + inside)

    def piece_copy(k, c, source=None):
        return pltpu.make_async_remote_copy(
            src_ref=comm.at[k, c] if source is None else source.at[:, :, :, pl.ds(c * f_piece, f_piece)],
            dst_ref=comm.at[k + 1, c],
            send_sem=block_send.at[k, c], recv_sem=block_recv.at[k, c],
            device_id={"chan": chan - 1}, device_id_type=MESH)

    def scale_copy(k):
        return pltpu.make_async_remote_copy(
            src_ref=scales.at[k], dst_ref=scales.at[k + 1],
            send_sem=scale_send.at[k], recv_sem=scale_recv.at[k],
            device_id={"chan": chan - 1}, device_id_type=MESH)

    @pl.when(chan > 0)
    def _():
        for c in range(EARLY):
            piece_copy(0, c, spec_ref).start()

    for load in loads:
        load.wait()

    for w in range(w_dev):
        total = None
        for c in range(PIECES):
            x = comm[0, c, w].astype(jnp.float32)
            s = x[0] * x[0] + x[1] * x[1]
            for q in range(f_piece // LANES):
                term = s[:, q * LANES:(q + 1) * LANES]
                total = term if total is None else total + term
        power[w] = total

    power_copies = []
    for step in range(1, n_freq):
        copy = pltpu.make_async_remote_copy(
            src_ref=power, dst_ref=power_in.at[step - 1],
            send_sem=power_send.at[step - 1], recv_sem=power_recv.at[step - 1],
            device_id={"freq": lax.rem(freq + step, n_freq)}, device_id_type=MESH)
        copy.start()
        power_copies.append(copy)

    for copy in power_copies:
        copy.wait()

    lane = lax.broadcasted_iota(jnp.int32, (ch_dev, LANES), 1)
    tile = jnp.zeros((ch_dev, LANES), jnp.float32)
    for w in range(w_dev):
        total = power[w]
        for step in range(1, n_freq):
            total = total + power_in[step - 1, w]
        mean = jnp.sum(total, axis=-1, keepdims=True) / (f_dev * n_freq)
        tile = jnp.where(lane == w, lax.rsqrt(mean + EPS), tile)
    scales[0] = tile

    @pl.when(chan > 0)
    def _():
        scale_copy(0).start()
        for c in range(EARLY, PIECES):
            piece_copy(0, c, spec_ref).start()

    def spread(k):
        tile = scales[k]
        for w in range(w_dev):
            gains[w] = jnp.broadcast_to(tile[:, w:w + 1], (ch_dev, LANES))

    spread(0)
    for w in range(w_dev):
        gain = jnp.concatenate([gains[w]] * (f_piece // LANES), axis=1)
        kept = keep_ref[w].astype(jnp.float32)
        for c in range(PIECES):
            white = (comm[0, c, w].astype(jnp.float32) * gain[None]).astype(jnp.bfloat16)
            own[w, :, :, pl.ds(c * f_piece, f_piece)] = white.astype(jnp.float32) * kept

    for load in tables:
        load.wait()

    def make_table(a, carry):
        fine_cos, fine_sin = fine[0], fine[1]
        coarse_cos, coarse_sin = coarse[0, pl.ds(a, 1)], coarse[1, pl.ds(a, 1)]
        cos = coarse_cos * fine_cos - coarse_sin * fine_sin
        minus_sin = -(coarse_sin * fine_cos) - coarse_cos * fine_sin
        per = LANES // FINE
        row = pl.multiple_of((a // per) * (2 * LANES) + lax.rem(a, per) * FINE, FINE)
        for value, at in ((cos, row), (minus_sin, row + LANES)):
            high, low = split(value)
            at = pl.ds(pl.multiple_of(at, FINE), FINE)
            table[0, at] = high
            table[1, at] = low
        return carry

    lax.fori_loop(0, groups, make_table, 0)

    def sum_copy(k, step):
        g, where = peer(step)
        return pltpu.make_async_remote_copy(
            src_ref=partial.at[k, g], dst_ref=arrived.at[k, step - 1],
            send_sem=sum_send.at[k, step - 1], recv_sem=sum_recv.at[k, step - 1],
            device_id=where, device_id_type=MESH)

    def receive(k, pieces, with_scale):
        @pl.when(chan + k < n_chan)
        def _():
            onward = jnp.logical_and(k < reach, chan > 0)
            for c in pieces:
                piece_copy(k - 1, c).wait_recv()

                @pl.when(onward)
                def _():
                    piece_copy(k, c).start()

            if with_scale:
                scale_copy(k - 1).wait_recv()

                @pl.when(onward)
                def _():
                    scale_copy(k).start()

    def compute(k, first, last):
        start = first * f_piece
        depth = (last - first) * f_piece

        def cross(q, c):
            lanes = pl.ds(pl.multiple_of(start + q * LANES, LANES), LANES)
            per = f_piece // LANES
            piece = first + q // per
            within = pl.ds(pl.multiple_of(lax.rem(q, per) * LANES, LANES), LANES)
            partner = []
            for w in range(w_dev):
                white = comm[k, piece, w, :, :, within].astype(jnp.float32) * gains[w][None]
                partner.append(white.astype(jnp.bfloat16).astype(jnp.float32))
            for i in range(0, ch_dev, 2):
                real, imag = [], []
                for ii in (i, i + 1):
                    re = im = None
                    for w in range(w_dev):
                        a = jnp.broadcast_to(own[w, 0, pl.ds(ii, 1), lanes], (ch_dev, LANES))
                        b = jnp.broadcast_to(own[w, 1, pl.ds(ii, 1), lanes], (ch_dev, LANES))
                        p, r = partner[w][0], partner[w][1]
                        one, two = a * p + b * r, b * p - a * r
                        re = one if re is None else re + one
                        im = two if im is None else im + two
                    real.append(re)
                    imag.append(im)
                for part, value in enumerate((real, imag)):
                    high, low = split(jnp.concatenate(value, axis=0))
                    at = pl.ds(pl.multiple_of(2 * start + q * 2 * LANES + part * LANES, LANES), LANES)
                    lhs[pl.ds(i * ch_dev, 2 * ch_dev), at] = high
                    lhs[pl.ds(rows + i * ch_dev, 2 * ch_dev), at] = low
            return c

        lax.fori_loop(0, depth // LANES, cross, 0)
        deep = pl.ds(2 * start, 2 * depth)
        for step in list(range(1, n_group)) + [0]:
            g, _ = peer(step)
            lags = pl.ds(pl.multiple_of(g * lag_dev, lag_dev), lag_dev)
            both = jnp.dot(lhs[:, deep], table[0, deep, lags], preferred_element_type=jnp.float32)
            rest = jnp.dot(lhs[pl.ds(0, rows), deep], table[1, deep, lags], preferred_element_type=jnp.float32)
            value = both[:rows] + (both[rows:] + rest)
            partial[k, g] = value if first == 0 else partial[k, g] + value
            if step and last == PIECES:
                sum_copy(k, step).start()

    def finish(k):
        @pl.when(chan + k < n_chan)
        def _():
            total = partial[k, me]
            for step in range(1, n_group):
                sum_copy(k, step).wait_recv()
                total = total + arrived[k, step - 1]
            for c in range(ch_dev):
                out_ref[c, k] = total[c * ch_dev:(c + 1) * ch_dev] * (mask_ref[k, c].astype(jnp.float32) * scale)

        @pl.when(chan + k >= n_chan)
        def _():
            out_ref[:, k] = jnp.zeros((ch_dev, ch_dev, lag_dev), jnp.float32)

    receive(1, range(EARLY), True)

    def one_offset(k, carry):
        @pl.when(chan + k < n_chan)
        def _():
            spread(k)
            compute(k, 0, EARLY)

        for c in range(EARLY, PIECES):
            @pl.when(k > 0)
            def _():
                receive(k, (c,), False)

            @pl.when(chan + k < n_chan)
            def _():
                compute(k, c, c + 1)

        @pl.when(k > 0)
        def _():
            @pl.when(k < reach)
            def _():
                receive(k + 1, range(EARLY), True)

            finish(k - 1)

        return carry

    lax.fori_loop(0, reach + 1, one_offset, 0)
    finish(reach)

    for k in range(reach + 1):
        @pl.when(chan + k < n_chan)
        def _():
            for step in range(1, n_group):
                sum_copy(k, step).wait_send()

        if k < reach:
            @pl.when(jnp.logical_and(chan > 0, chan + k < n_chan))
            def _():
                scale_copy(k).wait_send()
                for c in range(PIECES):
                    piece_copy(k, c, spec_ref if k == 0 else None).wait_send()


def local(spectra, keep, pair_mask):
    w_dev, _, ch_dev, f_dev = spectra.shape
    reach = pair_mask.shape[1] - 1
    n_chan, n_freq, n_win = (lax.axis_size(name) for name in ("chan", "freq", "win"))
    n_group = n_freq * n_win
    lag_dev = LAGS // n_group
    rows = ch_dev * ch_dev
    coarse = jnp.asarray(turn_table(F_LO + np.arange(0, f_dev * n_freq, FINE)))
    fine = jnp.asarray(turn_table(np.arange(FINE)))
    groups = f_dev // FINE
    smem = pl.BlockSpec(memory_space=pltpu.SMEM)
    hbm = pl.BlockSpec(memory_space=pl.ANY)
    dma = pltpu.SemaphoreType.DMA
    return pl.pallas_call(
        functools.partial(kernel, reach, (n_chan, n_win, n_freq)),
        out_shape=pltpu.VMEM((ch_dev, reach + 1, ch_dev, lag_dev), jnp.float32),
        in_specs=[smem, smem, hbm, hbm, hbm],
        out_specs=pl.BlockSpec(memory_space=pltpu.VMEM),
        scratch_shapes=[
            pltpu.VMEM((reach + 1, PIECES, w_dev, 2, ch_dev, f_dev // PIECES), jnp.bfloat16),
            pltpu.VMEM((reach + 1, ch_dev, LANES), jnp.float32),
            pltpu.VMEM((w_dev, ch_dev, LANES), jnp.float32),
            pltpu.VMEM(spectra.shape, jnp.float32),
            pltpu.VMEM((w_dev, ch_dev, LANES), jnp.float32),
            pltpu.VMEM((n_freq - 1, w_dev, ch_dev, LANES), jnp.float32),
            pltpu.VMEM((2, groups, LAGS), jnp.float32),
            pltpu.VMEM((2, FINE, LAGS), jnp.float32),
            pltpu.VMEM((2, 2 * f_dev, LAGS), jnp.bfloat16),
            pltpu.VMEM((2 * rows, 2 * f_dev), jnp.bfloat16),
            pltpu.VMEM((reach + 1, n_group, rows, lag_dev), jnp.float32),
            pltpu.VMEM((reach + 1, n_group - 1, rows, lag_dev), jnp.float32),
            dma((PIECES,)),
            dma((2,)),
            dma((n_freq - 1,)),
            dma((n_freq - 1,)),
            dma((reach,)),
            dma((reach,)),
            dma((reach, PIECES)),
            dma((reach, PIECES)),
            dma((reach + 1, n_group - 1)),
            dma((reach + 1, n_group - 1)),
        ],
        compiler_params=pltpu.CompilerParams(
            collective_id=0, has_side_effects=True, vmem_limit_bytes=60 * 1024 * 1024),
    )(keep, pair_mask.T, spectra, coarse, fine)


def solution(mesh):
    in_specs = (
        P("win", None, ("fibre", "chan"), "freq"),
        P(("fibre", "win")),
        P(("fibre", "chan"), None),
    )
    out_specs = P(("fibre", "chan"), None, None, ("win", "freq"))
    return jax.shard_map(local, mesh=mesh, in_specs=in_specs, out_specs=out_specs, check_vma=False)
```

```python
import functools
import math

import jax
import jax.numpy as jnp
import numpy as np
from jax import lax
from jax.experimental import pallas as pl
from jax.experimental.pallas import tpu as pltpu
from jax.sharding import PartitionSpec as P

LAGS = 1024
F_LO = 60
NSAMP = 15000
EPS = 1e-06
LANES = 128
FINE = 16
PIECES = 2
EARLY = 1
MESH = pl.DeviceIdType.MESH


def turn_table(bins):
    offsets = np.arange(LAGS, dtype=np.int64) - LAGS // 2
    turns = np.remainder(np.asarray(bins, np.int64)[:, None] * offsets[None, :], NSAMP)
    angle = turns.astype(np.float64) * (2.0 * math.pi / NSAMP)
    return np.stack([np.cos(angle), np.sin(angle)]).astype(np.float32)


def split(x):
    high = x.astype(jnp.bfloat16)
    low = (x - high.astype(jnp.float32)).astype(jnp.bfloat16)
    return high, low


def kernel(reach, sizes, keep_ref, mask_ref, spec_ref, coarse_ref, fine_ref, out_ref,
           comm, scales, gains, own, power, power_in, coarse, fine, table, lhs, partial, arrived,
           spec_sem, load_sem, power_send, power_recv, scale_send, scale_recv, block_send, block_recv, sum_send, sum_recv):
    n_chan, n_win, n_freq = sizes
    w_dev, _, ch_dev, f_dev = spec_ref.shape
    chan, win, freq = (lax.axis_index(name) for name in ("chan", "win", "freq"))
    n_group = n_win * n_freq
    me = win * n_freq + freq
    lag_dev = LAGS // n_group
    rows = ch_dev * ch_dev
    f_piece = f_dev // PIECES
    scale = 1.0 / math.sqrt(w_dev * n_win * f_dev * n_freq)

    def peer(step):
        to_win = lax.rem(win + step // n_freq, n_win)
        to_freq = lax.rem(freq + step % n_freq, n_freq)
        return to_win * n_freq + to_freq, {"win": to_win, "freq": to_freq}

    barrier = pltpu.get_barrier_semaphore()

    @pl.when(chan > 0)
    def _():
        pl.semaphore_signal(barrier, inc=1, device_id={"chan": chan - 1}, device_id_type=MESH)

    @pl.when(chan < n_chan - 1)
    def _():
        pl.semaphore_signal(barrier, inc=1, device_id={"chan": chan + 1}, device_id_type=MESH)

    for step in range(1, n_group):
        pl.semaphore_signal(barrier, inc=1, device_id=peer(step)[1], device_id_type=MESH)

    groups = f_dev // FINE
    loads = [pltpu.make_async_copy(
        spec_ref.at[:, :, :, pl.ds(c * f_piece, f_piece)], comm.at[0, c], spec_sem.at[c]) for c in range(PIECES)]
    tables = [
        pltpu.make_async_copy(
            coarse_ref.at[:, pl.ds(pl.multiple_of(freq * groups, groups), groups)], coarse, load_sem.at[0]),
        pltpu.make_async_copy(fine_ref, fine, load_sem.at[1])]
    for load in loads + tables:
        load.start()

    inside = jnp.where(chan > 0, 1, 0) + jnp.where(chan < n_chan - 1, 1, 0)
    pl.semaphore_wait(barrier, n_group - 1 + inside)

    def piece_copy(k, c, source=None):
        return pltpu.make_async_remote_copy(
            src_ref=comm.at[k, c] if source is None else source.at[:, :, :, pl.ds(c * f_piece, f_piece)],
            dst_ref=comm.at[k + 1, c],
            send_sem=block_send.at[k, c], recv_sem=block_recv.at[k, c],
            device_id={"chan": chan - 1}, device_id_type=MESH)

    def scale_copy(k):
        return pltpu.make_async_remote_copy(
            src_ref=scales.at[k], dst_ref=scales.at[k + 1],
            send_sem=scale_send.at[k], recv_sem=scale_recv.at[k],
            device_id={"chan": chan - 1}, device_id_type=MESH)

    @pl.when(chan > 0)
    def _():
        for c in range(EARLY):
            piece_copy(0, c, spec_ref).start()

    for load in loads:
        load.wait()

    for w in range(w_dev):
        total = None
        for c in range(PIECES):
            x = comm[0, c, w].astype(jnp.float32)
            s = x[0] * x[0] + x[1] * x[1]
            for q in range(f_piece // LANES):
                term = s[:, q * LANES:(q + 1) * LANES]
                total = term if total is None else total + term
        power[w] = total

    power_copies = []
    for step in range(1, n_freq):
        copy = pltpu.make_async_remote_copy(
            src_ref=power, dst_ref=power_in.at[step - 1],
            send_sem=power_send.at[step - 1], recv_sem=power_recv.at[step - 1],
            device_id={"freq": lax.rem(freq + step, n_freq)}, device_id_type=MESH)
        copy.start()
        power_copies.append(copy)

    for copy in power_copies:
        copy.wait()

    lane = lax.broadcasted_iota(jnp.int32, (ch_dev, LANES), 1)
    tile = jnp.zeros((ch_dev, LANES), jnp.float32)
    for w in range(w_dev):
        total = power[w]
        for step in range(1, n_freq):
            total = total + power_in[step - 1, w]
        mean = jnp.sum(total, axis=-1, keepdims=True) / (f_dev * n_freq)
        tile = jnp.where(lane == w, lax.rsqrt(mean + EPS), tile)
    scales[0] = tile

    @pl.when(chan > 0)
    def _():
        scale_copy(0).start()
        for c in range(EARLY, PIECES):
            piece_copy(0, c, spec_ref).start()

    def spread(k):
        tile = scales[k]
        for w in range(w_dev):
            gains[w] = jnp.broadcast_to(tile[:, w:w + 1], (ch_dev, LANES))

    spread(0)
    for w in range(w_dev):
        gain = jnp.concatenate([gains[w]] * (f_piece // LANES), axis=1)
        kept = keep_ref[w].astype(jnp.float32)
        for c in range(PIECES):
            white = (comm[0, c, w].astype(jnp.float32) * gain[None]).astype(jnp.bfloat16)
            own[w, :, :, pl.ds(c * f_piece, f_piece)] = white.astype(jnp.float32) * kept

    for load in tables:
        load.wait()

    def make_table(a, carry):
        fine_cos, fine_sin = fine[0], fine[1]
        coarse_cos, coarse_sin = coarse[0, pl.ds(a, 1)], coarse[1, pl.ds(a, 1)]
        cos = coarse_cos * fine_cos - coarse_sin * fine_sin
        minus_sin = -(coarse_sin * fine_cos) - coarse_cos * fine_sin
        per = LANES // FINE
        row = pl.multiple_of((a // per) * (2 * LANES) + lax.rem(a, per) * FINE, FINE)
        for value, at in ((cos, row), (minus_sin, row + LANES)):
            high, low = split(value)
            at = pl.ds(pl.multiple_of(at, FINE), FINE)
            table[0, at] = high
            table[1, at] = low
        return carry

    lax.fori_loop(0, groups, make_table, 0)

    def sum_copy(k, step):
        g, where = peer(step)
        return pltpu.make_async_remote_copy(
            src_ref=partial.at[k, g], dst_ref=arrived.at[k, step - 1],
            send_sem=sum_send.at[k, step - 1], recv_sem=sum_recv.at[k, step - 1],
            device_id=where, device_id_type=MESH)

    def receive(k, pieces, with_scale):
        @pl.when(chan + k < n_chan)
        def _():
            onward = jnp.logical_and(k < reach, chan > 0)
            for c in pieces:
                piece_copy(k - 1, c).wait_recv()

                @pl.when(onward)
                def _():
                    piece_copy(k, c).start()

            if with_scale:
                scale_copy(k - 1).wait_recv()

                @pl.when(onward)
                def _():
                    scale_copy(k).start()

    def compute(k, first, last):
        start = first * f_piece
        depth = (last - first) * f_piece

        def cross(q, c):
            lanes = pl.ds(pl.multiple_of(start + q * LANES, LANES), LANES)
            per = f_piece // LANES
            piece = first + q // per
            within = pl.ds(pl.multiple_of(lax.rem(q, per) * LANES, LANES), LANES)
            partner = []
            for w in range(w_dev):
                white = comm[k, piece, w, :, :, within].astype(jnp.float32) * gains[w][None]
                partner.append(white.astype(jnp.bfloat16).astype(jnp.float32))
            for i in range(0, ch_dev, 2):
                real, imag = [], []
                for ii in (i, i + 1):
                    re = im = None
                    for w in range(w_dev):
                        a = jnp.broadcast_to(own[w, 0, pl.ds(ii, 1), lanes], (ch_dev, LANES))
                        b = jnp.broadcast_to(own[w, 1, pl.ds(ii, 1), lanes], (ch_dev, LANES))
                        p, r = partner[w][0], partner[w][1]
                        one, two = a * p + b * r, b * p - a * r
                        re = one if re is None else re + one
                        im = two if im is None else im + two
                    real.append(re)
                    imag.append(im)
                for part, value in enumerate((real, imag)):
                    high, low = split(jnp.concatenate(value, axis=0))
                    at = pl.ds(pl.multiple_of(2 * start + q * 2 * LANES + part * LANES, LANES), LANES)
                    lhs[pl.ds(i * ch_dev, 2 * ch_dev), at] = high
                    lhs[pl.ds(rows + i * ch_dev, 2 * ch_dev), at] = low
            return c

        lax.fori_loop(0, depth // LANES, cross, 0)
        deep = pl.ds(2 * start, 2 * depth)
        for step in [*range(n_freq, n_group), *range(1, n_freq), 0]:
            g, _ = peer(step)
            lags = pl.ds(pl.multiple_of(g * lag_dev, lag_dev), lag_dev)
            both = jnp.dot(lhs[:, deep], table[0, deep, lags], preferred_element_type=jnp.float32)
            rest = jnp.dot(lhs[pl.ds(0, rows), deep], table[1, deep, lags], preferred_element_type=jnp.float32)
            value = both[:rows] + (both[rows:] + rest)
            partial[k, g] = value if first == 0 else partial[k, g] + value
            if step and last == PIECES:
                sum_copy(k, step).start()

    def finish(k):
        @pl.when(chan + k < n_chan)
        def _():
            total = partial[k, me]
            for step in range(1, n_group):
                sum_copy(k, step).wait_recv()
                total = total + arrived[k, step - 1]
            for c in range(ch_dev):
                out_ref[c, k] = total[c * ch_dev:(c + 1) * ch_dev] * (mask_ref[k, c].astype(jnp.float32) * scale)

        @pl.when(chan + k >= n_chan)
        def _():
            out_ref[:, k] = jnp.zeros((ch_dev, ch_dev, lag_dev), jnp.float32)

    receive(1, range(EARLY), True)

    def one_offset(k, carry):
        @pl.when(chan + k < n_chan)
        def _():
            spread(k)
            compute(k, 0, EARLY)

        for c in range(EARLY, PIECES):
            @pl.when(k > 0)
            def _():
                receive(k, (c,), False)

            @pl.when(chan + k < n_chan)
            def _():
                compute(k, c, c + 1)

        @pl.when(k > 0)
        def _():
            @pl.when(k < reach)
            def _():
                receive(k + 1, range(EARLY), True)

            finish(k - 1)

        return carry

    lax.fori_loop(0, reach + 1, one_offset, 0)
    finish(reach)

    for k in range(reach + 1):
        @pl.when(chan + k < n_chan)
        def _():
            for step in range(1, n_group):
                sum_copy(k, step).wait_send()

        if k < reach:
            @pl.when(jnp.logical_and(chan > 0, chan + k < n_chan))
            def _():
                scale_copy(k).wait_send()
                for c in range(PIECES):
                    piece_copy(k, c, spec_ref if k == 0 else None).wait_send()


def local(spectra, keep, pair_mask):
    w_dev, _, ch_dev, f_dev = spectra.shape
    reach = pair_mask.shape[1] - 1
    n_chan, n_freq, n_win = (lax.axis_size(name) for name in ("chan", "freq", "win"))
    n_group = n_freq * n_win
    lag_dev = LAGS // n_group
    rows = ch_dev * ch_dev
    coarse = jnp.asarray(turn_table(F_LO + np.arange(0, f_dev * n_freq, FINE)))
    fine = jnp.asarray(turn_table(np.arange(FINE)))
    groups = f_dev // FINE
    smem = pl.BlockSpec(memory_space=pltpu.SMEM)
    hbm = pl.BlockSpec(memory_space=pl.ANY)
    dma = pltpu.SemaphoreType.DMA
    return pl.pallas_call(
        functools.partial(kernel, reach, (n_chan, n_win, n_freq)),
        out_shape=pltpu.VMEM((ch_dev, reach + 1, ch_dev, lag_dev), jnp.float32),
        in_specs=[smem, smem, hbm, hbm, hbm],
        out_specs=pl.BlockSpec(memory_space=pltpu.VMEM),
        scratch_shapes=[
            pltpu.VMEM((reach + 1, PIECES, w_dev, 2, ch_dev, f_dev // PIECES), jnp.bfloat16),
            pltpu.VMEM((reach + 1, ch_dev, LANES), jnp.float32),
            pltpu.VMEM((w_dev, ch_dev, LANES), jnp.float32),
            pltpu.VMEM(spectra.shape, jnp.float32),
            pltpu.VMEM((w_dev, ch_dev, LANES), jnp.float32),
            pltpu.VMEM((n_freq - 1, w_dev, ch_dev, LANES), jnp.float32),
            pltpu.VMEM((2, groups, LAGS), jnp.float32),
            pltpu.VMEM((2, FINE, LAGS), jnp.float32),
            pltpu.VMEM((2, 2 * f_dev, LAGS), jnp.bfloat16),
            pltpu.VMEM((2 * rows, 2 * f_dev), jnp.bfloat16),
            pltpu.VMEM((reach + 1, n_group, rows, lag_dev), jnp.float32),
            pltpu.VMEM((reach + 1, n_group - 1, rows, lag_dev), jnp.float32),
            dma((PIECES,)),
            dma((2,)),
            dma((n_freq - 1,)),
            dma((n_freq - 1,)),
            dma((reach,)),
            dma((reach,)),
            dma((reach, PIECES)),
            dma((reach, PIECES)),
            dma((reach + 1, n_group - 1)),
            dma((reach + 1, n_group - 1)),
        ],
        compiler_params=pltpu.CompilerParams(
            collective_id=0, has_side_effects=True, vmem_limit_bytes=60 * 1024 * 1024),
    )(keep, pair_mask.T, spectra, coarse, fine)


def solution(mesh):
    in_specs = (
        P("win", None, ("fibre", "chan"), "freq"),
        P(("fibre", "win")),
        P(("fibre", "chan"), None),
    )
    out_specs = P(("fibre", "chan"), None, None, ("win", "freq"))
    return jax.shard_map(local, mesh=mesh, in_specs=in_specs, out_specs=out_specs, check_vma=False)
```
